128 devices in a mesh: row: 4 (over x), col: 32 (over y, z, core).
Axes of the slice: x: 4, y: 4, z: 4, core: 2. Of those that a mesh axis runs over, the one named last changes fastest.
Arguments:
- object_slices: float32 [4, 2, 2048, 8192], P(None, None, 'row', 'col'), may hold values from -4 to 4
- probe_wave: float32 [2, 256, 256], replicated, may hold values from -5 to 5
- propagator_phase: float32 [256, 256], replicated, may hold values from -3.140625 to 3.140625
- positions: int32 [384, 2], P(('row', 'col')), may hold values from 0 to 511, as said below
- slot_count: int32 [128], P(('row', 'col')), may hold values from 1 to 3, as said below
- intensity: float32 [384, 256, 256], P(('row', 'col')), may hold values from 0 to 2
Outputs:
- object_grad: float32 [4, 2, 2048, 8192], P(None, None, 'row', 'col')
- probe_grad: float32 [2, 256, 256], replicated
The draws below stay inside these ranges and needn't reach their ends.
Inputs may be any that keep to these rules, and one draw needn't show every extreme that they name: positions[g, 0] is below 512 and positions[g, 1] below 256; slots are ordered by owner device, owners in row-major order of the mesh. Slot k of owner d is in use when k < slot_count[d].
All inputs are finite; a program needn't handle non-finite values.
Results may differ from the reference program's by a relative error of at most 0.0002.
Values sent between devices are 32-bit elements; how exact they have to be, the bound alone decides.
No kernel may reach another device: no remote copies, remote signals or barrier semaphores. Data moves between devices by JAX's collectives and lax.ppermute only.
A program may use at most 128 MiB of HBM per device.

```python
import jax
import jax.numpy as jnp
from jax import lax

WIN = 256
SLICES = 4
TILE_ROWS = 512
TILE_COLS = 256
SLOTS_DEV = 3
TILES = 128
SLOTS = 384
OBJ_ROWS = 2048
OBJ_COLS = 8192
N_COL = 32


def draw_positions(key, part):
    key_rows = jax.random.fold_in(key, 11)
    key_cols = jax.random.fold_in(key, 12)
    key_pick = jax.random.fold_in(key, 13)
    row_offsets = jax.random.randint(key_rows, (SLOTS,), 0, TILE_ROWS)
    col_offsets = jax.random.randint(key_cols, (SLOTS,), 0, TILE_COLS)
    chosen = jax.random.randint(key_pick, (), 0, SLOTS)
    other = (chosen + 1) % SLOTS
    row_offsets = row_offsets.at[chosen].set(TILE_ROWS - 1).at[other].set(0)
    col_offsets = col_offsets.at[chosen].set(TILE_COLS - 1).at[other].set(0)
    return jnp.stack([row_offsets, col_offsets], axis=1).astype(jnp.int32)


def draw_slot_count(key, part):
    key_count = jax.random.fold_in(key, 21)
    key_pick = jax.random.fold_in(key, 22)
    counts = jax.random.randint(key_count, (TILES,), 1, SLOTS_DEV + 1)
    chosen = jax.random.randint(key_pick, (), 0, TILES)
    other = (chosen + 1) % TILES
    counts = counts.at[chosen].set(SLOTS_DEV).at[other].set(1)
    return counts.astype(jnp.int32)


def block_levels(rng, shape, cuts, low, top_value):
    def one(dim, blocks):
        steps = jax.random.uniform(jax.random.fold_in(jax.random.fold_in(rng, 6), dim), (blocks,), jnp.float32, low / len(cuts), top_value / len(cuts))
        return jnp.repeat(jnp.exp(steps), shape[dim] // blocks).reshape((-1,) + (1,) * (len(shape) - dim - 1))

    level = one(*cuts[0])
    for cut in cuts[1:]:
        level = level * one(*cut)
    return level


def normal_values(stream_key, dims, scale, bound, shards=(), held_as=jnp.bfloat16):
    factor_of = block_levels(stream_key, dims, shards, -0.22, 0.18) if shards else 1.0
    entries = jax.random.normal(stream_key, dims, jnp.float32) * scale * factor_of
    return jnp.minimum(jnp.maximum(entries, -bound), bound).astype(held_as)


def setup_inputs(seed: int = 0) -> dict:
    splits = jax.random.split(jax.random.key(seed), 7)
    object_slices = normal_values(splits[0], (SLICES, 2, OBJ_ROWS, OBJ_COLS), 0.7, 4.0, ((2, 4), (3, 32)), jnp.float32)
    probe_wave = normal_values(splits[1], (2, WIN, WIN), 1.0, 5.0, (), jnp.float32)
    propagator_phase = jnp.clip(jax.random.uniform(splits[2], (WIN, WIN), jnp.float32, -3.140625, 3.140625), -3.140625, 3.140625)
    positions = draw_positions(jax.random.fold_in(splits[6], 71), 0)
    slot_count = draw_slot_count(jax.random.fold_in(splits[6], 71), 0)
    intensity = jnp.clip(2.0 * jax.random.uniform(splits[5], (SLOTS, WIN, WIN), jnp.float32) ** block_levels(splits[5], (SLOTS, WIN, WIN), ((0, 128),), -0.2, 0.2), 0.0, 2.0)
    return dict(object_slices=object_slices, probe_wave=probe_wave, propagator_phase=propagator_phase, positions=positions, slot_count=slot_count, intensity=intensity)


def slot_misfit(window, probe_wave, propagator_phase, measured, slot_used):
    slab = window[:, 0] + 1j * window[:, 1]
    wave = probe_wave[0] + 1j * probe_wave[1]
    kernel = jnp.cos(propagator_phase) + 1j * jnp.sin(propagator_phase)
    exit_wave = wave * slab[0]
    for layer in range(SLICES):
        exit_wave = wave * slab[layer]
        if layer < SLICES - 1:
            wave = jnp.fft.ifft2(kernel * jnp.fft.fft2(exit_wave, norm='ortho'), norm='ortho')
    far_field = jnp.fft.fft2(exit_wave, norm='ortho')
    far_power = jnp.real(far_field) ** 2 + jnp.imag(far_field) ** 2
    residual = far_power - measured
    return 0.25 * slot_used * jnp.sum(residual * residual)

def reference(object_slices, probe_wave, propagator_phase, positions, slot_count, intensity):
    padded = jnp.pad(object_slices, ((0, 0), (0, 0), (0, WIN), (0, WIN)))
    slot_ids = jnp.arange(SLOTS, dtype=jnp.int32)
    owner_dev = slot_ids // SLOTS_DEV
    row_start = (owner_dev // N_COL * TILE_ROWS + positions[:, 0]).astype(jnp.int32)
    col_start = (owner_dev % N_COL * TILE_COLS + positions[:, 1]).astype(jnp.int32)
    in_use = (slot_ids % SLOTS_DEV < slot_count[owner_dev]).astype(object_slices.dtype)
    grad_fn = jax.grad(slot_misfit, argnums=(0, 1))
    anchor = jnp.zeros((), jnp.int32)

    def visit_slot(totals, slot_data):
        grad_obj, grad_probe = totals
        top_row, left_col, slot_used, measured = slot_data
        corner = (anchor, anchor, top_row, left_col)
        window = lax.dynamic_slice(padded, corner, (SLICES, 2, WIN, WIN))
        grad_win, grad_wave = grad_fn(window, probe_wave, propagator_phase, measured, slot_used)
        current = lax.dynamic_slice(grad_obj, corner, (SLICES, 2, WIN, WIN))
        grad_obj = lax.dynamic_update_slice(grad_obj, current + grad_win, corner)
        return ((grad_obj, grad_probe + grad_wave), None)
    initial = (jnp.zeros_like(padded), jnp.zeros_like(probe_wave))
    finals, unused = lax.scan(visit_slot, initial, (row_start, col_start, in_use, intensity))
    grad_obj, grad_probe = finals
    return (grad_obj[:, :, :OBJ_ROWS, :OBJ_COLS], grad_probe)
```

```python
import functools
import math

import jax
import jax.numpy as jnp
import numpy as np
from jax import lax
from jax.experimental import pallas as pl
from jax.experimental.pallas import tpu as pltpu
from jax.sharding import PartitionSpec as P


WIN = 256
HALF = 128
F32 = jnp.float32
BF16 = jnp.bfloat16


def shift(x, axis, by):
    devices = lax.axis_size(axis)
    pairs = [(i, i + by) for i in range(devices) if 0 <= i + by < devices]
    return lax.ppermute(x, axis, pairs)


def dft_tables():
    n = np.arange(HALF)
    even = 2.0 * math.pi * ((2 * np.outer(n, n)) % WIN) / WIN
    odd = 2.0 * math.pi * ((np.outer(n, 2 * n + 1)) % WIN) / WIN
    tables = []
    for angle in (even, odd):
        cos, sin = np.cos(angle) / 16.0, np.sin(angle) / 16.0
        table = np.block([[cos, -sin], [sin, cos]])
        tables += [table, table.T]
    whole = np.stack(tables).astype(np.float32)
    high = whole.astype(jnp.bfloat16)
    low = (whole - high.astype(np.float32)).astype(jnp.bfloat16)
    return np.stack([high, low], axis=1)


def split(x):
    high = x.astype(BF16)
    low = (x - high.astype(F32)).astype(BF16)
    return high, low


def right_mul(x, tab, index):
    high, low = split(x)
    t_high, t_low = tab[index, 0], tab[index, 1]
    return jnp.dot(
        jnp.concatenate([high, low, high], axis=1),
        jnp.concatenate([t_high, t_high, t_low], axis=0),
        preferred_element_type=F32,
    )


def left_mul(x, tab, index):
    high, low = split(x)
    t_high, t_low = tab[index, 0], tab[index, 1]
    return jnp.dot(
        jnp.concatenate([t_high, t_high, t_low], axis=1),
        jnp.concatenate([high, low, high], axis=0),
        preferred_element_type=F32,
    )


EVEN, EVEN_T, ODD, ODD_T = range(4)


def forward2d(re, im, tab):
    re0, re1, im0, im1 = re[:, :HALF], re[:, HALF:], im[:, :HALF], im[:, HALF:]
    even = right_mul(jnp.concatenate([re0 + re1, im0 + im1], axis=1), tab, EVEN)
    odd = right_mul(jnp.concatenate([re0 - re1, im0 - im1], axis=1), tab, ODD)
    re = jnp.concatenate([even[:, :HALF], odd[:, :HALF]], axis=1)
    im = jnp.concatenate([even[:, HALF:], odd[:, HALF:]], axis=1)
    re0, re1, im0, im1 = re[:HALF], re[HALF:], im[:HALF], im[HALF:]
    even = left_mul(jnp.concatenate([re0 + re1, im0 + im1], axis=0), tab, EVEN_T)
    odd = left_mul(jnp.concatenate([re0 - re1, im0 - im1], axis=0), tab, ODD_T)
    return even, odd


def inverse2d(even, odd, tab):
    a = left_mul(even, tab, EVEN)
    b = left_mul(odd, tab, ODD)
    plus, minus = a + b, a - b
    re = jnp.concatenate([plus[:HALF], minus[:HALF]], axis=0)
    im = jnp.concatenate([plus[HALF:], minus[HALF:]], axis=0)
    a = right_mul(jnp.concatenate([re[:, :HALF], im[:, :HALF]], axis=1), tab, EVEN_T)
    b = right_mul(jnp.concatenate([re[:, HALF:], im[:, HALF:]], axis=1), tab, ODD_T)
    plus, minus = a + b, a - b
    re = jnp.concatenate([plus[:, :HALF], minus[:, :HALF]], axis=1)
    im = jnp.concatenate([plus[:, HALF:], minus[:, HALF:]], axis=1)
    return re, im


def propagate(re, im, tab, kern, sign):
    halves = forward2d(re, im, tab)
    moved = []
    for parity in range(2):
        f_re, f_im = halves[parity][:HALF], halves[parity][HALF:]
        k_re, k_im = kern[parity, 0], kern[parity, 1] * sign
        moved.append(
            jnp.concatenate([k_re * f_re - k_im * f_im, k_re * f_im + k_im * f_re], axis=0)
        )
    return inverse2d(moved[0], moved[1], tab)


def far_adjoint(re, im, tab, measured, used):
    halves = forward2d(re, im, tab)
    moved = []
    for parity in range(2):
        f_re, f_im = halves[parity][:HALF], halves[parity][HALF:]
        weight = (f_re * f_re + f_im * f_im - measured[0, parity]) * used
        moved.append(jnp.concatenate([weight * f_re, weight * f_im], axis=0))
    return inverse2d(moved[0], moved[1], tab)


def cut(ext, part, row, col):
    base = col // HALF
    lane = col % HALF
    keep = lax.broadcasted_iota(jnp.int32, (WIN, HALF), 1) < HALF - lane
    back = (HALF - lane) % HALF
    turned = [pltpu.roll(ext[part, base + j, pl.ds(row, WIN), :], back, 1) for j in range(3)]
    return jnp.concatenate(
        [jnp.where(keep, turned[0], turned[1]), jnp.where(keep, turned[1], turned[2])], axis=1
    )


def add_back(ext, part, row, col, value):
    base = col // HALF
    lane = col % HALF
    keep = lax.broadcasted_iota(jnp.int32, (WIN, HALF), 1) >= lane
    zero = jnp.zeros((WIN, HALF), F32)
    turned = [pltpu.roll(value[:, j * HALF : (j + 1) * HALF], lane, 1) for j in range(2)]
    wide = [
        jnp.where(keep, turned[0], zero),
        jnp.where(keep, turned[1], turned[0]),
        jnp.where(keep, zero, turned[1]),
    ]
    for j in range(3):
        place = (part, base + j, pl.ds(row, WIN), slice(None))
        ext[place] = ext[place] + wide[j]


def gather_ext(own, right, lower, corner, ext):
    for j in range(2):
        lanes = slice(j * HALF, (j + 1) * HALF)
        ext[:, j, :512] = own[:, :, lanes]
        ext[:, 2 + j, :512] = right[:, :, lanes]
        ext[:, j, 512:] = lower[:, :, lanes]
        ext[:, 2 + j, 512:] = corner[:, :, lanes]


def spread_ext(ext, own, right, lower, corner):
    for j in range(2):
        lanes = slice(j * HALF, (j + 1) * HALF)
        own[:, :, lanes] = ext[:, j, :512]
        right[:, :, lanes] = ext[:, 2 + j, :512]
        lower[:, :, lanes] = ext[:, j, 512:]
        corner[:, :, lanes] = ext[:, 2 + j, 512:]


def forward_kernel(pos, own, right, lower, corner, wave, tab, kern, slab_out, wave_out, ext):
    slot = pl.program_id(0)

    @pl.when(slot == 0)
    def _():
        gather_ext(own, right, lower, corner, ext)

    row, col = pos[slot, 0], pos[slot, 1]
    s_re, s_im = cut(ext, 0, row, col), cut(ext, 1, row, col)
    slab_out[0, 0], slab_out[0, 1] = s_re, s_im
    w_re, w_im = wave[0, 0], wave[0, 1]
    wave_out[0, 0], wave_out[0, 1] = propagate(
        w_re * s_re - w_im * s_im, w_re * s_im + w_im * s_re, tab, kern, 1.0
    )


def turn_kernel(pos, count, own, right, lower, corner, wave, tab, measured,
                g_own, g_right, g_lower, g_corner, g_wave, ext, g_ext):
    slot = pl.program_id(0)

    @pl.when(slot == 0)
    def _():
        gather_ext(own, right, lower, corner, ext)
        g_ext[...] = jnp.zeros(g_ext.shape, F32)

    row, col = pos[slot, 0], pos[slot, 1]
    used = jnp.where(slot < count[0], 1.0, 0.0).astype(F32)
    s_re, s_im = cut(ext, 0, row, col), cut(ext, 1, row, col)
    w_re, w_im = wave[0, 0], wave[0, 1]
    e_re, e_im = far_adjoint(
        w_re * s_re - w_im * s_im, w_re * s_im + w_im * s_re, tab, measured, used
    )
    add_back(g_ext, 0, row, col, w_re * e_re + w_im * e_im)
    add_back(g_ext, 1, row, col, w_re * e_im - w_im * e_re)
    g_wave[0, 0] = s_re * e_re + s_im * e_im
    g_wave[0, 1] = s_re * e_im - s_im * e_re

    @pl.when(slot == pl.num_programs(0) - 1)
    def _():
        spread_ext(g_ext, g_own, g_right, g_lower, g_corner)


def backward_kernel(first, pos, slab, wave, g_next, tab, kern,
                    g_own, g_right, g_lower, g_corner, g_wave, g_ext):
    slot = pl.program_id(0)

    @pl.when(slot == 0)
    def _():
        g_ext[...] = jnp.zeros(g_ext.shape, F32)
        if first:
            g_wave[...] = jnp.zeros(g_wave.shape, F32)

    row, col = pos[slot, 0], pos[slot, 1]
    s_re, s_im = slab[0, 0], slab[0, 1]
    w_re, w_im = wave[0, 0], wave[0, 1]
    e_re, e_im = propagate(g_next[0, 0], g_next[0, 1], tab, kern, -1.0)
    add_back(g_ext, 0, row, col, w_re * e_re + w_im * e_im)
    add_back(g_ext, 1, row, col, w_re * e_im - w_im * e_re)
    p_re = s_re * e_re + s_im * e_im
    p_im = s_re * e_im - s_im * e_re
    if first:
        g_wave[0, 0] += p_re
        g_wave[0, 1] += p_im
    else:
        g_wave[0, 0], g_wave[0, 1] = p_re, p_im

    @pl.when(slot == pl.num_programs(0) - 1)
    def _():
        spread_ext(g_ext, g_own, g_right, g_lower, g_corner)


def whole(*shape):
    return pl.BlockSpec(shape, lambda slot, *_: (0,) * len(shape))


def by_slot(*shape):
    return pl.BlockSpec((1,) + shape, lambda slot, *_: (slot,) + (0,) * len(shape))


TILE = (2, 512, 256)
STRIP = (2, 256, 256)
PARAMS = pltpu.CompilerParams(dimension_semantics=("arbitrary",), vmem_limit_bytes=56 << 20)
COST = pl.CostEstimate(flops=3 * 24 * 2 * 256**3, bytes_accessed=12 << 20, transcendentals=0)
EXT = pltpu.VMEM((2, 4, 768, HALF), F32)


def arr(*shape):
    return jax.ShapeDtypeStruct(shape, F32)


def run_forward(slots, pos, parts, wave, tab, kern):
    shared = wave.shape[0] == 1
    return pl.pallas_call(
        forward_kernel,
        grid_spec=pltpu.PrefetchScalarGridSpec(
            num_scalar_prefetch=1,
            grid=(slots,),
            in_specs=[whole(*TILE), whole(*TILE), whole(*STRIP), whole(*STRIP),
                      whole(1, *STRIP) if shared else by_slot(*STRIP),
                      whole(4, 2, 256, 256), whole(2, 2, 128, 256)],
            out_specs=[by_slot(*STRIP), by_slot(*STRIP)],
            scratch_shapes=[EXT],
        ),
        out_shape=[arr(slots, *STRIP), arr(slots, *STRIP)],
        compiler_params=PARAMS,
        cost_estimate=COST,
        name="forward",
    )(pos, *parts, wave, tab, kern)


def run_turn(slots, pos, count, parts, wave, tab, measured):
    return pl.pallas_call(
        turn_kernel,
        grid_spec=pltpu.PrefetchScalarGridSpec(
            num_scalar_prefetch=2,
            grid=(slots,),
            in_specs=[whole(*TILE), whole(*TILE), whole(*STRIP), whole(*STRIP),
                      by_slot(*STRIP), whole(4, 2, 256, 256), by_slot(2, 128, 256)],
            out_specs=[whole(*TILE), whole(*TILE), whole(*STRIP), whole(*STRIP), by_slot(*STRIP)],
            scratch_shapes=[EXT, EXT],
        ),
        out_shape=[arr(*TILE), arr(*TILE), arr(*STRIP), arr(*STRIP), arr(slots, *STRIP)],
        compiler_params=PARAMS,
        cost_estimate=COST,
        name="turn",
    )(pos, count, *parts, wave, tab, measured)


def run_backward(slots, pos, slab, wave, g_next, tab, kern, first):
    shared = wave.shape[0] == 1
    return pl.pallas_call(
        functools.partial(backward_kernel, first),
        grid_spec=pltpu.PrefetchScalarGridSpec(
            num_scalar_prefetch=1,
            grid=(slots,),
            in_specs=[by_slot(*STRIP), whole(1, *STRIP) if shared else by_slot(*STRIP),
                      by_slot(*STRIP), whole(4, 2, 256, 256), whole(2, 2, 128, 256)],
            out_specs=[whole(*TILE), whole(*TILE), whole(*STRIP), whole(*STRIP),
                       whole(1, *STRIP) if first else by_slot(*STRIP)],
            scratch_shapes=[EXT],
        ),
        out_shape=[arr(*TILE), arr(*TILE), arr(*STRIP), arr(*STRIP),
                   arr(1 if first else slots, *STRIP)],
        compiler_params=PARAMS,
        cost_estimate=COST,
        name="backward",
    )(pos, slab, wave, g_next, tab, kern)


def parity_order(x):
    order = np.concatenate([np.arange(0, WIN, 2), np.arange(1, WIN, 2)])
    pick = jnp.asarray(np.eye(WIN, dtype=np.float32)[order])
    high = lax.Precision.HIGHEST
    x = jnp.einsum("...rc,dc->...rd", x, pick, precision=high)
    return jnp.einsum("er,...rd->...ed", pick, x, precision=high)


def sum_over_devices(x):
    shape = x.shape
    part = x.reshape(512, 256)
    steps = []
    for axis in ("col", "row"):
        bit = 1
        while bit < lax.axis_size(axis):
            steps.append((axis, bit))
            bit *= 2

    def swap(value, axis, bit):
        return lax.ppermute(value, axis, [(i, i ^ bit) for i in range(lax.axis_size(axis))])

    for axis, bit in steps:
        upper = (lax.axis_index(axis) // bit) % 2 == 1
        half = part.shape[0] // 2
        low, high = part[:half], part[half:]
        part = jnp.where(upper, high, low) + swap(jnp.where(upper, low, high), axis, bit)
    for axis, bit in reversed(steps):
        upper = (lax.axis_index(axis) // bit) % 2 == 1
        other = swap(part, axis, bit)
        part = jnp.where(
            upper, jnp.concatenate([other, part]), jnp.concatenate([part, other])
        )
    return part.reshape(shape)


def per_device(object_slices, probe_wave, propagator_phase, positions, slot_count, intensity):
    layers = object_slices.shape[0]
    slots = positions.shape[0]
    tab = jnp.asarray(dft_tables())
    phase = parity_order(propagator_phase).reshape(2, 1, HALF, WIN)
    kern = jnp.concatenate([jnp.cos(phase), jnp.sin(phase)], axis=1)
    measured = parity_order(intensity).reshape(slots, 2, HALF, WIN)
    parts = []
    for layer in range(layers):
        own = object_slices[layer]
        lower = shift(own[:, :WIN], "row", -1)
        right = shift(own, "col", -1)
        corner = shift(lower, "col", -1)
        parts.append((own, right, lower, corner))
    waves = [probe_wave[None]]
    slabs = []
    for layer in range(layers - 1):
        slab, wave = run_forward(slots, positions, parts[layer], waves[layer], tab, kern)
        slabs.append(slab)
        waves.append(wave)
    grads = [None] * layers
    out = run_turn(slots, positions, slot_count, parts[layers - 1], waves[layers - 1], tab, measured)
    grads[layers - 1], g_wave = out[:4], out[4]
    for layer in reversed(range(layers - 1)):
        out = run_backward(
            slots, positions, slabs[layer], waves[layer], g_wave, tab, kern, layer == 0
        )
        grads[layer], g_wave = out[:4], out[4]
    tiles = []
    for layer in range(layers):
        g_own, g_right, g_lower, g_corner = grads[layer]
        own = g_own + shift(g_right, "col", 1)
        lower = shift(g_lower + shift(g_corner, "col", 1), "row", 1)
        tiles.append(own.at[:, :WIN].add(lower))
    return (jnp.stack(tiles), sum_over_devices(g_wave[0]))


def solution(mesh):
    placed = (
        P(None, None, "row", "col"),
        P(),
        P(),
        P(("row", "col"), None),
        P(("row", "col")),
        P(("row", "col"), None, None),
    )
    return jax.shard_map(
        per_device,
        mesh=mesh,
        in_specs=placed,
        out_specs=(P(None, None, "row", "col"), P()),
        check_vma=False,
    )
```

```python
import functools
import math

import jax
import jax.numpy as jnp
import numpy as np
from jax import lax
from jax.experimental import pallas as pl
from jax.experimental.pallas import tpu as pltpu
from jax.sharding import PartitionSpec as P


WIN = 256
HALF = 128
F32 = jnp.float32
BF16 = jnp.bfloat16


def shift(x, axis, by):
    devices = lax.axis_size(axis)
    pairs = [(i, i + by) for i in range(devices) if 0 <= i + by < devices]
    return lax.ppermute(x, axis, pairs)


def dft_tables():
    n = np.arange(HALF)
    even = 2.0 * math.pi * ((2 * np.outer(n, n)) % WIN) / WIN
    odd = 2.0 * math.pi * ((np.outer(n, 2 * n + 1)) % WIN) / WIN
    tables = []
    for angle in (even, odd):
        cos, sin = np.cos(angle) / 16.0, np.sin(angle) / 16.0
        table = np.block([[cos, -sin], [sin, cos]])
        tables += [table, table.T]
    whole = np.stack(tables).astype(np.float32)
    high = whole.astype(jnp.bfloat16)
    low = (whole - high.astype(np.float32)).astype(jnp.bfloat16)
    return np.stack([high, low], axis=1)


def split(x):
    high = x.astype(BF16)
    low = (x - high.astype(F32)).astype(BF16)
    return high, low


def right_mul(x, tab, index):
    high, low = split(x)
    t_high, t_low = tab[index, 0], tab[index, 1]
    return jnp.dot(
        jnp.concatenate([high, low, high], axis=1),
        jnp.concatenate([t_high, t_high, t_low], axis=0),
        preferred_element_type=F32,
    )


def left_mul(x, tab, index):
    high, low = split(x)
    t_high, t_low = tab[index, 0], tab[index, 1]
    return jnp.dot(
        jnp.concatenate([t_high, t_high, t_low], axis=1),
        jnp.concatenate([high, low, high], axis=0),
        preferred_element_type=F32,
    )


EVEN, EVEN_T, ODD, ODD_T = range(4)


def forward2d(re, im, tab):
    re0, re1, im0, im1 = re[:, :HALF], re[:, HALF:], im[:, :HALF], im[:, HALF:]
    even = right_mul(jnp.concatenate([re0 + re1, im0 + im1], axis=1), tab, EVEN)
    odd = right_mul(jnp.concatenate([re0 - re1, im0 - im1], axis=1), tab, ODD)
    re = jnp.concatenate([even[:, :HALF], odd[:, :HALF]], axis=1)
    im = jnp.concatenate([even[:, HALF:], odd[:, HALF:]], axis=1)
    re0, re1, im0, im1 = re[:HALF], re[HALF:], im[:HALF], im[HALF:]
    even = left_mul(jnp.concatenate([re0 + re1, im0 + im1], axis=0), tab, EVEN_T)
    odd = left_mul(jnp.concatenate([re0 - re1, im0 - im1], axis=0), tab, ODD_T)
    return even, odd


def inverse2d(even, odd, tab):
    a = left_mul(even, tab, EVEN)
    b = left_mul(odd, tab, ODD)
    plus, minus = a + b, a - b
    re = jnp.concatenate([plus[:HALF], minus[:HALF]], axis=0)
    im = jnp.concatenate([plus[HALF:], minus[HALF:]], axis=0)
    a = right_mul(jnp.concatenate([re[:, :HALF], im[:, :HALF]], axis=1), tab, EVEN_T)
    b = right_mul(jnp.concatenate([re[:, HALF:], im[:, HALF:]], axis=1), tab, ODD_T)
    plus, minus = a + b, a - b
    re = jnp.concatenate([plus[:, :HALF], minus[:, :HALF]], axis=1)
    im = jnp.concatenate([plus[:, HALF:], minus[:, HALF:]], axis=1)
    return re, im


def propagate(re, im, tab, kern, sign):
    halves = forward2d(re, im, tab)
    moved = []
    for parity in range(2):
        f_re, f_im = halves[parity][:HALF], halves[parity][HALF:]
        k_re, k_im = kern[parity, 0], kern[parity, 1] * sign
        moved.append(
            jnp.concatenate([k_re * f_re - k_im * f_im, k_re * f_im + k_im * f_re], axis=0)
        )
    return inverse2d(moved[0], moved[1], tab)


def far_adjoint(re, im, tab, measured, used):
    halves = forward2d(re, im, tab)
    moved = []
    for parity in range(2):
        f_re, f_im = halves[parity][:HALF], halves[parity][HALF:]
        weight = (f_re * f_re + f_im * f_im - measured[0, parity]) * used
        moved.append(jnp.concatenate([weight * f_re, weight * f_im], axis=0))
    return inverse2d(moved[0], moved[1], tab)


def cut(ext, part, row, col):
    base = col // HALF
    lane = col % HALF
    keep = lax.broadcasted_iota(jnp.int32, (WIN, HALF), 1) < HALF - lane
    back = (HALF - lane) % HALF
    turned = [pltpu.roll(ext[part, base + j, pl.ds(row, WIN), :], back, 1) for j in range(3)]
    return jnp.concatenate(
        [jnp.where(keep, turned[0], turned[1]), jnp.where(keep, turned[1], turned[2])], axis=1
    )


def add_back(ext, part, row, col, value):
    base = col // HALF
    lane = col % HALF
    keep = lax.broadcasted_iota(jnp.int32, (WIN, HALF), 1) >= lane
    zero = jnp.zeros((WIN, HALF), F32)
    turned = [pltpu.roll(value[:, j * HALF : (j + 1) * HALF], lane, 1) for j in range(2)]
    wide = [
        jnp.where(keep, turned[0], zero),
        jnp.where(keep, turned[1], turned[0]),
        jnp.where(keep, zero, turned[1]),
    ]
    for j in range(3):
        place = (part, base + j, pl.ds(row, WIN), slice(None))
        ext[place] = ext[place] + wide[j]


def gather_ext(own, lower, sides, ext):
    for j in range(2):
        lanes = slice(j * HALF, (j + 1) * HALF)
        ext[:, j, :512] = own[0, :, :, lanes]
        ext[:, j, 512:] = lower[:, :, lanes]
        top = 0
        for side in sides:
            rows = side.shape[1]
            ext[:, 2 + j, top : top + rows] = side[:, :, lanes]
            top += rows


def spread_ext(ext, own, lower, sides):
    for j in range(2):
        lanes = slice(j * HALF, (j + 1) * HALF)
        own[:, :, lanes] = ext[:, j, :512]
        lower[:, :, lanes] = ext[:, j, 512:]
        top = 0
        for side in sides:
            rows = side.shape[1]
            side[:, :, lanes] = ext[:, 2 + j, top : top + rows]
            top += rows


def forward_kernel(side_count, pos, own, lower, *refs):
    sides, (wave, tab, kern, slab_out, wave_out, ext) = refs[:side_count], refs[side_count:]
    slot = pl.program_id(0)

    @pl.when(slot == 0)
    def _():
        gather_ext(own, lower, sides, ext)

    row, col = pos[slot, 0], pos[slot, 1]
    s_re, s_im = cut(ext, 0, row, col), cut(ext, 1, row, col)
    slab_out[0, 0], slab_out[0, 1] = s_re, s_im
    w_re, w_im = wave[0, 0], wave[0, 1]
    wave_out[0, 0], wave_out[0, 1] = propagate(
        w_re * s_re - w_im * s_im, w_re * s_im + w_im * s_re, tab, kern, 1.0
    )


def turn_kernel(side_count, pos, count, own, lower, *refs):
    sides, (wave, tab, measured, g_own, g_lower, g_side, g_wave, ext, g_ext) = (
        refs[:side_count], refs[side_count:]
    )
    slot = pl.program_id(0)

    @pl.when(slot == 0)
    def _():
        gather_ext(own, lower, sides, ext)
        g_ext[...] = jnp.zeros(g_ext.shape, F32)

    row, col = pos[slot, 0], pos[slot, 1]
    used = jnp.where(slot < count[0], 1.0, 0.0).astype(F32)
    s_re, s_im = cut(ext, 0, row, col), cut(ext, 1, row, col)
    w_re, w_im = wave[0, 0], wave[0, 1]
    e_re, e_im = far_adjoint(
        w_re * s_re - w_im * s_im, w_re * s_im + w_im * s_re, tab, measured, used
    )
    add_back(g_ext, 0, row, col, w_re * e_re + w_im * e_im)
    add_back(g_ext, 1, row, col, w_re * e_im - w_im * e_re)
    g_wave[0, 0] = s_re * e_re + s_im * e_im
    g_wave[0, 1] = s_re * e_im - s_im * e_re

    @pl.when(slot == pl.num_programs(0) - 1)
    def _():
        spread_ext(g_ext, g_own, g_lower, [g_side])


def backward_kernel(first, pos, slab, wave, g_next, tab, kern, g_own, g_lower, *refs):
    sides, (g_wave, g_ext) = refs[:-2], refs[-2:]
    slot = pl.program_id(0)

    @pl.when(slot == 0)
    def _():
        g_ext[...] = jnp.zeros(g_ext.shape, F32)
        if first:
            g_wave[...] = jnp.zeros(g_wave.shape, F32)

    row, col = pos[slot, 0], pos[slot, 1]
    s_re, s_im = slab[0, 0], slab[0, 1]
    w_re, w_im = wave[0, 0], wave[0, 1]
    e_re, e_im = propagate(g_next[0, 0], g_next[0, 1], tab, kern, -1.0)
    add_back(g_ext, 0, row, col, w_re * e_re + w_im * e_im)
    add_back(g_ext, 1, row, col, w_re * e_im - w_im * e_re)
    p_re = s_re * e_re + s_im * e_im
    p_im = s_re * e_im - s_im * e_re
    if first:
        g_wave[0, 0] += p_re
        g_wave[0, 1] += p_im
    else:
        g_wave[0, 0], g_wave[0, 1] = p_re, p_im

    @pl.when(slot == pl.num_programs(0) - 1)
    def _():
        spread_ext(g_ext, g_own, g_lower, sides)


def whole(*shape):
    return pl.BlockSpec(shape, lambda slot, *_: (0,) * len(shape))


def by_slot(*shape):
    return pl.BlockSpec((1,) + shape, lambda slot, *_: (slot,) + (0,) * len(shape))


TILE = (2, 512, 256)
STRIP = (2, 256, 256)
SIDE = (2, 768, 256)
PARAMS = pltpu.CompilerParams(dimension_semantics=("arbitrary",), vmem_limit_bytes=56 << 20)
COST = pl.CostEstimate(flops=10 * 1000 * 1000 * 1000, bytes_accessed=12 << 20, transcendentals=0)
EXT = pltpu.VMEM((2, 4, 768, HALF), F32)
TABLES = (4, 2, 256, 256)


def arr(*shape):
    return jax.ShapeDtypeStruct(shape, F32)


def tile_of(layer):
    return pl.BlockSpec((1,) + TILE, lambda slot, *_: (layer, 0, 0, 0))


def run_forward(layer, slots, pos, tiles, lower, sides, wave, tab, kern):
    shared = wave.shape[0] == 1
    return pl.pallas_call(
        functools.partial(forward_kernel, len(sides)),
        grid_spec=pltpu.PrefetchScalarGridSpec(
            num_scalar_prefetch=1,
            grid=(slots,),
            in_specs=[tile_of(layer), whole(*STRIP), *[whole(*side.shape) for side in sides],
                      whole(1, *STRIP) if shared else by_slot(*STRIP),
                      whole(*TABLES), whole(2, 2, HALF, WIN)],
            out_specs=[by_slot(*STRIP), by_slot(*STRIP)],
            scratch_shapes=[EXT],
        ),
        out_shape=[arr(slots, *STRIP), arr(slots, *STRIP)],
        compiler_params=PARAMS,
        cost_estimate=COST,
        name="forward",
    )(pos, tiles, lower, *sides, wave, tab, kern)


def run_turn(layer, slots, pos, count, tiles, lower, sides, wave, tab, measured):
    return pl.pallas_call(
        functools.partial(turn_kernel, len(sides)),
        grid_spec=pltpu.PrefetchScalarGridSpec(
            num_scalar_prefetch=2,
            grid=(slots,),
            in_specs=[tile_of(layer), whole(*STRIP), *[whole(*side.shape) for side in sides],
                      by_slot(*STRIP), whole(*TABLES), by_slot(2, HALF, WIN)],
            out_specs=[whole(*TILE), whole(*STRIP), whole(*SIDE), by_slot(*STRIP)],
            scratch_shapes=[EXT, EXT],
        ),
        out_shape=[arr(*TILE), arr(*STRIP), arr(*SIDE), arr(slots, *STRIP)],
        compiler_params=PARAMS,
        cost_estimate=COST,
        name="turn",
    )(pos, count, tiles, lower, *sides, wave, tab, measured)


def run_backward(slots, pos, slab, wave, g_next, tab, kern, first):
    shared = wave.shape[0] == 1
    sides = [TILE, STRIP] if first else [SIDE]
    return pl.pallas_call(
        functools.partial(backward_kernel, first),
        grid_spec=pltpu.PrefetchScalarGridSpec(
            num_scalar_prefetch=1,
            grid=(slots,),
            in_specs=[by_slot(*STRIP), whole(1, *STRIP) if shared else by_slot(*STRIP),
                      by_slot(*STRIP), whole(*TABLES), whole(2, 2, HALF, WIN)],
            out_specs=[whole(*TILE), whole(*STRIP), *[whole(*side) for side in sides],
                       whole(1, *STRIP) if first else by_slot(*STRIP)],
            scratch_shapes=[EXT],
        ),
        out_shape=[arr(*TILE), arr(*STRIP), *[arr(*side) for side in sides],
                   arr(1 if first else slots, *STRIP)],
        compiler_params=PARAMS,
        cost_estimate=COST,
        name="backward",
    )(pos, slab, wave, g_next, tab, kern)


def parity_order(x):
    order = np.concatenate([np.arange(0, WIN, 2), np.arange(1, WIN, 2)])
    pick = jnp.asarray(np.eye(WIN, dtype=np.float32)[order])
    high = lax.Precision.HIGHEST
    x = jnp.einsum("...rc,dc->...rd", x, pick, precision=high)
    return jnp.einsum("er,...rd->...ed", pick, x, precision=high)


def turn_by(x, axis, by):
    sizes = {"x": lax.axis_size("row"), "y": 4, "z": 4, "core": 2}
    pairs = []
    for x_at in range(sizes["x"]):
        for y_at in range(4):
            for z_at in range(4):
                for core in range(2):
                    place = {"x": x_at, "y": y_at, "z": z_at, "core": core}
                    there = dict(place)
                    there[axis] = (place[axis] + by) % sizes[axis]
                    pairs.append(tuple(
                        p["x"] * 32 + p["y"] * 8 + p["z"] * 2 + p["core"] for p in (place, there)
                    ))
    return lax.ppermute(x, ("row", "col"), pairs)


def sum_over_devices(x):
    shape = x.shape
    part = x.reshape(512, 256)
    col = lax.axis_index("col")
    place = {"core": (col % 2, 2), "y": (col // 8, 4)}
    for axis in ("core", "y"):
        me, size = place[axis]
        rows = part.shape[0] // size
        total = lax.dynamic_slice_in_dim(part, me * rows, rows)
        for by in range(1, size):
            block = lax.dynamic_slice_in_dim(part, (me + by) % size * rows, rows)
            other = turn_by(block, axis, by)
            total = total + other
        part = total
    for axis in ("x", "z"):
        others = [turn_by(part, axis, by) for by in (1, 2, 3)]
        part = part + others[0] + others[1] + others[2]
    for axis in ("y", "core"):
        me, size = place[axis]
        rows = part.shape[0]
        joined = jnp.zeros((rows * size, 256), F32)
        joined = lax.dynamic_update_slice_in_dim(joined, part, me * rows, 0)
        for by in range(1, size):
            other = turn_by(part, axis, by)
            joined = lax.dynamic_update_slice_in_dim(
                joined, other, (me - by) % size * rows, 0
            )
        part = joined
    return part.reshape(shape)


def work(tiles, probe_wave, propagator_phase, positions, slot_count, intensity):
    layers = tiles.shape[0]
    slots = positions.shape[0]
    last = layers - 1
    strip = tiles[0, :, :WIN]
    lowers = [shift(strip, "row", -1)]
    rest, strip = lax.optimization_barrier((tiles, strip))
    right = shift(rest[0], "col", -1)
    for layer in range(1, layers):
        lowers.append(shift(rest[layer, :, :WIN], "row", -1))
    tab = jnp.asarray(dft_tables())
    phase = parity_order(propagator_phase).reshape(2, 1, HALF, WIN)
    kern = jnp.concatenate([jnp.cos(phase), jnp.sin(phase)], axis=1)
    measured = parity_order(intensity).reshape(slots, 2, HALF, WIN)
    corner = shift(lowers[0], "col", -1)
    sides = [(right, corner)]
    for layer in range(1, layers):
        joined = jnp.concatenate([rest[layer], lowers[layer]], axis=1)
        sides.append((shift(joined, "col", -1),))
    waves = [probe_wave[None]]
    slabs = []
    for layer in range(last):
        slab, wave = run_forward(
            layer, slots, positions, tiles, lowers[layer], sides[layer], waves[layer], tab, kern
        )
        slabs.append(slab)
        waves.append(wave)
    grads = [None] * layers
    *grads[last], g_wave = run_turn(
        last, slots, positions, slot_count, tiles, lowers[last], sides[last], waves[last],
        tab, measured
    )
    for layer in reversed(range(last)):
        *grads[layer], g_wave = run_backward(
            slots, positions, slabs[layer], waves[layer], g_wave, tab, kern, layer == 0
        )
    outs = [None] * layers
    for layer in reversed(range(layers)):
        own, lower, *side = grads[layer]
        if layer:
            back = shift(side[0], "col", 1)
            right, corner = back[:, :512], back[:, 512:]
        else:
            corner = shift(side[1], "col", 1)
            right = shift(side[0], "col", 1)
        below = shift(lower + corner, "row", 1)
        outs[layer] = (own + right).at[:, :WIN].add(below)
    probe = sum_over_devices(g_wave[0])
    return (jnp.stack(outs), probe)


def solution(mesh):
    placed = (
        P(None, None, "row", "col"),
        P(),
        P(),
        P(("row", "col"), None),
        P(("row", "col")),
        P(("row", "col"), None, None),
    )
    return jax.shard_map(
        work,
        mesh=mesh,
        in_specs=placed,
        out_specs=(P(None, None, "row", "col"), P()),
        check_vma=False,
    )
```

```python
import functools
import math

import jax
import jax.numpy as jnp
import numpy as np
from jax import lax
from jax.experimental import pallas as pl
from jax.experimental.pallas import tpu as pltpu
from jax.sharding import PartitionSpec as P


WIN = 256
HALF = 128
F32 = jnp.float32
BF16 = jnp.bfloat16


def shift(x, axis, by):
    devices = lax.axis_size(axis)
    pairs = [(i, i + by) for i in range(devices) if 0 <= i + by < devices]
    return lax.ppermute(x, axis, pairs)


def dft_tables():
    n = np.arange(HALF)
    even = 2.0 * math.pi * ((2 * np.outer(n, n)) % WIN) / WIN
    odd = 2.0 * math.pi * ((np.outer(n, 2 * n + 1)) % WIN) / WIN
    tables = []
    for angle in (even, odd):
        cos, sin = np.cos(angle) / 16.0, np.sin(angle) / 16.0
        tables.append(np.block([[cos, -sin], [sin, cos]]))
    whole = np.stack(tables).astype(np.float32)
    high = whole.astype(jnp.bfloat16)
    low = (whole - high.astype(np.float32)).astype(jnp.bfloat16)
    held = lax.optimization_barrier(jnp.asarray(np.stack([high, low], axis=1)))
    return jnp.stack([held, held.transpose(0, 1, 3, 2)], axis=1).reshape(4, 2, WIN, WIN)


def split(x):
    high = x.astype(BF16)
    low = (x - high.astype(F32)).astype(BF16)
    return high, low


def right_mul(x, tab, index):
    high, low = split(x)
    t_high, t_low = tab[index, 0], tab[index, 1]
    return jnp.dot(
        jnp.concatenate([high, low, high], axis=1),
        jnp.concatenate([t_high, t_high, t_low], axis=0),
        preferred_element_type=F32,
    )


def left_mul(x, tab, index):
    high, low = split(x)
    t_high, t_low = tab[index, 0], tab[index, 1]
    return jnp.dot(
        jnp.concatenate([t_high, t_high, t_low], axis=1),
        jnp.concatenate([high, low, high], axis=0),
        preferred_element_type=F32,
    )


EVEN, EVEN_T, ODD, ODD_T = range(4)


def forward2d(re, im, tab):
    re0, re1, im0, im1 = re[:, :HALF], re[:, HALF:], im[:, :HALF], im[:, HALF:]
    even = right_mul(jnp.concatenate([re0 + re1, im0 + im1], axis=1), tab, EVEN)
    odd = right_mul(jnp.concatenate([re0 - re1, im0 - im1], axis=1), tab, ODD)
    re = jnp.concatenate([even[:, :HALF], odd[:, :HALF]], axis=1)
    im = jnp.concatenate([even[:, HALF:], odd[:, HALF:]], axis=1)
    re0, re1, im0, im1 = re[:HALF], re[HALF:], im[:HALF], im[HALF:]
    even = left_mul(jnp.concatenate([re0 + re1, im0 + im1], axis=0), tab, EVEN_T)
    odd = left_mul(jnp.concatenate([re0 - re1, im0 - im1], axis=0), tab, ODD_T)
    return even, odd


def inverse2d(even, odd, tab):
    a = left_mul(even, tab, EVEN)
    b = left_mul(odd, tab, ODD)
    plus, minus = a + b, a - b
    re = jnp.concatenate([plus[:HALF], minus[:HALF]], axis=0)
    im = jnp.concatenate([plus[HALF:], minus[HALF:]], axis=0)
    a = right_mul(jnp.concatenate([re[:, :HALF], im[:, :HALF]], axis=1), tab, EVEN_T)
    b = right_mul(jnp.concatenate([re[:, HALF:], im[:, HALF:]], axis=1), tab, ODD_T)
    plus, minus = a + b, a - b
    re = jnp.concatenate([plus[:, :HALF], minus[:, :HALF]], axis=1)
    im = jnp.concatenate([plus[:, HALF:], minus[:, HALF:]], axis=1)
    return re, im


def propagate(re, im, tab, kern, sign):
    halves = forward2d(re, im, tab)
    moved = []
    for parity in range(2):
        f_re, f_im = halves[parity][:HALF], halves[parity][HALF:]
        k_re, k_im = kern[parity, 0], kern[parity, 1] * sign
        moved.append(
            jnp.concatenate([k_re * f_re - k_im * f_im, k_re * f_im + k_im * f_re], axis=0)
        )
    return inverse2d(moved[0], moved[1], tab)


def far_adjoint(re, im, tab, measured, used):
    halves = forward2d(re, im, tab)
    moved = []
    for parity in range(2):
        f_re, f_im = halves[parity][:HALF], halves[parity][HALF:]
        weight = (f_re * f_re + f_im * f_im - measured[0, parity]) * used
        moved.append(jnp.concatenate([weight * f_re, weight * f_im], axis=0))
    return inverse2d(moved[0], moved[1], tab)


def cut(ext, part, row, col):
    base = col // HALF
    lane = col % HALF
    keep = lax.broadcasted_iota(jnp.int32, (WIN, HALF), 1) < HALF - lane
    back = (HALF - lane) % HALF
    turned = [pltpu.roll(ext[part, base + j, pl.ds(row, WIN), :], back, 1) for j in range(3)]
    return jnp.concatenate(
        [jnp.where(keep, turned[0], turned[1]), jnp.where(keep, turned[1], turned[2])], axis=1
    )


def add_back(ext, part, row, col, value):
    base = col // HALF
    lane = col % HALF
    keep = lax.broadcasted_iota(jnp.int32, (WIN, HALF), 1) >= lane
    zero = jnp.zeros((WIN, HALF), F32)
    turned = [pltpu.roll(value[:, j * HALF : (j + 1) * HALF], lane, 1) for j in range(2)]
    wide = [
        jnp.where(keep, turned[0], zero),
        jnp.where(keep, turned[1], turned[0]),
        jnp.where(keep, zero, turned[1]),
    ]
    for j in range(3):
        place = (part, base + j, pl.ds(row, WIN), slice(None))
        ext[place] = ext[place] + wide[j]


def gather_ext(own, lower, sides, ext):
    for j in range(2):
        lanes = slice(j * HALF, (j + 1) * HALF)
        ext[:, j, :512] = own[0, :, :, lanes]
        ext[:, j, 512:] = lower[:, :, lanes]
        top = 0
        for side in sides:
            rows = side.shape[1]
            ext[:, 2 + j, top : top + rows] = side[:, :, lanes]
            top += rows


def spread_ext(ext, own, lower, sides):
    for j in range(2):
        lanes = slice(j * HALF, (j + 1) * HALF)
        own[:, :, lanes] = ext[:, j, :512]
        lower[:, :, lanes] = ext[:, j, 512:]
        top = 0
        for side in sides:
            rows = side.shape[1]
            side[:, :, lanes] = ext[:, 2 + j, top : top + rows]
            top += rows


def forward_kernel(side_count, pos, own, lower, *refs):
    sides, (wave, tab, kern, slab_out, wave_out, ext) = refs[:side_count], refs[side_count:]
    slot = pl.program_id(0)

    @pl.when(slot == 0)
    def _():
        gather_ext(own, lower, sides, ext)

    row, col = pos[slot, 0], pos[slot, 1]
    s_re, s_im = cut(ext, 0, row, col), cut(ext, 1, row, col)
    slab_out[0, 0], slab_out[0, 1] = s_re, s_im
    w_re, w_im = wave[0, 0], wave[0, 1]
    wave_out[0, 0], wave_out[0, 1] = propagate(
        w_re * s_re - w_im * s_im, w_re * s_im + w_im * s_re, tab, kern, 1.0
    )


def turn_kernel(side_count, pos, count, own, lower, *refs):
    sides, (wave, tab, measured, g_own, g_lower, g_side, g_wave, ext, g_ext) = (
        refs[:side_count], refs[side_count:]
    )
    slot = pl.program_id(0)

    @pl.when(slot == 0)
    def _():
        gather_ext(own, lower, sides, ext)
        g_ext[...] = jnp.zeros(g_ext.shape, F32)

    row, col = pos[slot, 0], pos[slot, 1]
    used = jnp.where(slot < count[0], 1.0, 0.0).astype(F32)
    s_re, s_im = cut(ext, 0, row, col), cut(ext, 1, row, col)
    w_re, w_im = wave[0, 0], wave[0, 1]
    e_re, e_im = far_adjoint(
        w_re * s_re - w_im * s_im, w_re * s_im + w_im * s_re, tab, measured, used
    )
    add_back(g_ext, 0, row, col, w_re * e_re + w_im * e_im)
    add_back(g_ext, 1, row, col, w_re * e_im - w_im * e_re)
    g_wave[0, 0] = s_re * e_re + s_im * e_im
    g_wave[0, 1] = s_re * e_im - s_im * e_re

    @pl.when(slot == pl.num_programs(0) - 1)
    def _():
        spread_ext(g_ext, g_own, g_lower, [g_side])


def backward_kernel(first, pos, slab, wave, g_next, tab, kern, g_own, g_lower, *refs):
    sides, (g_wave, g_ext) = refs[:-2], refs[-2:]
    slot = pl.program_id(0)

    @pl.when(slot == 0)
    def _():
        g_ext[...] = jnp.zeros(g_ext.shape, F32)
        if first:
            g_wave[...] = jnp.zeros(g_wave.shape, F32)

    row, col = pos[slot, 0], pos[slot, 1]
    s_re, s_im = slab[0, 0], slab[0, 1]
    w_re, w_im = wave[0, 0], wave[0, 1]
    e_re, e_im = propagate(g_next[0, 0], g_next[0, 1], tab, kern, -1.0)
    add_back(g_ext, 0, row, col, w_re * e_re + w_im * e_im)
    add_back(g_ext, 1, row, col, w_re * e_im - w_im * e_re)
    p_re = s_re * e_re + s_im * e_im
    p_im = s_re * e_im - s_im * e_re
    if first:
        g_wave[0, 0] += p_re
        g_wave[0, 1] += p_im
    else:
        g_wave[0, 0], g_wave[0, 1] = p_re, p_im

    @pl.when(slot == pl.num_programs(0) - 1)
    def _():
        spread_ext(g_ext, g_own, g_lower, sides)


def whole(*shape):
    return pl.BlockSpec(shape, lambda slot, *_: (0,) * len(shape))


def by_slot(*shape):
    return pl.BlockSpec((1,) + shape, lambda slot, *_: (slot,) + (0,) * len(shape))


TILE = (2, 512, 256)
STRIP = (2, 256, 256)
SIDE = (2, 768, 256)
PARAMS = pltpu.CompilerParams(dimension_semantics=("arbitrary",), vmem_limit_bytes=26 << 20)
COST = pl.CostEstimate(flops=10 * 1000 * 1000 * 1000, bytes_accessed=12 << 20, transcendentals=0)
EXT = pltpu.VMEM((2, 4, 768, HALF), F32)
TABLES = (4, 2, 256, 256)


def arr(*shape):
    return jax.ShapeDtypeStruct(shape, F32)


def tile_of(layer):
    return pl.BlockSpec((1,) + TILE, lambda slot, *_: (layer, 0, 0, 0))


def run_forward(layer, slots, pos, tiles, lower, sides, wave, tab, kern):
    shared = wave.shape[0] == 1
    return pl.pallas_call(
        functools.partial(forward_kernel, len(sides)),
        grid_spec=pltpu.PrefetchScalarGridSpec(
            num_scalar_prefetch=1,
            grid=(slots,),
            in_specs=[tile_of(layer), whole(*STRIP), *[whole(*side.shape) for side in sides],
                      whole(1, *STRIP) if shared else by_slot(*STRIP),
                      whole(*TABLES), whole(2, 2, HALF, WIN)],
            out_specs=[by_slot(*STRIP), by_slot(*STRIP)],
            scratch_shapes=[EXT],
        ),
        out_shape=[arr(slots, *STRIP), arr(slots, *STRIP)],
        compiler_params=PARAMS,
        cost_estimate=COST,
        name="forward",
    )(pos, tiles, lower, *sides, wave, tab, kern)


def run_turn(layer, slots, pos, count, tiles, lower, sides, wave, tab, measured):
    return pl.pallas_call(
        functools.partial(turn_kernel, len(sides)),
        grid_spec=pltpu.PrefetchScalarGridSpec(
            num_scalar_prefetch=2,
            grid=(slots,),
            in_specs=[tile_of(layer), whole(*STRIP), *[whole(*side.shape) for side in sides],
                      by_slot(*STRIP), whole(*TABLES), by_slot(2, HALF, WIN)],
            out_specs=[whole(*TILE), whole(*STRIP), whole(*SIDE), by_slot(*STRIP)],
            scratch_shapes=[EXT, EXT],
        ),
        out_shape=[arr(*TILE), arr(*STRIP), arr(*SIDE), arr(slots, *STRIP)],
        compiler_params=PARAMS,
        cost_estimate=COST,
        name="turn",
    )(pos, count, tiles, lower, *sides, wave, tab, measured)


def run_backward(slots, pos, slab, wave, g_next, tab, kern, first):
    shared = wave.shape[0] == 1
    sides = [TILE, STRIP] if first else [SIDE]
    return pl.pallas_call(
        functools.partial(backward_kernel, first),
        grid_spec=pltpu.PrefetchScalarGridSpec(
            num_scalar_prefetch=1,
            grid=(slots,),
            in_specs=[by_slot(*STRIP), whole(1, *STRIP) if shared else by_slot(*STRIP),
                      by_slot(*STRIP), whole(*TABLES), whole(2, 2, HALF, WIN)],
            out_specs=[whole(*TILE), whole(*STRIP), *[whole(*side) for side in sides],
                       whole(1, *STRIP) if first else by_slot(*STRIP)],
            scratch_shapes=[EXT],
        ),
        out_shape=[arr(*TILE), arr(*STRIP), *[arr(*side) for side in sides],
                   arr(1 if first else slots, *STRIP)],
        compiler_params=PARAMS,
        cost_estimate=COST,
        name="backward",
    )(pos, slab, wave, g_next, tab, kern)


def parity_order(x):
    place = lax.broadcasted_iota(jnp.int32, (WIN, WIN), 0)
    source = lax.broadcasted_iota(jnp.int32, (WIN, WIN), 1)
    pick = (source == place % HALF * 2 + place // HALF).astype(F32)
    high = lax.Precision.HIGHEST
    x = jnp.einsum("...rc,dc->...rd", x, pick, precision=high)
    return jnp.einsum("er,...rd->...ed", pick, x, precision=high)


def permute_devices(x, there):
    count = lax.axis_size("row") * 32
    return lax.ppermute(x, ("row", "col"), [(i, there(i)) for i in range(count)])


def swap(x, axis, bit):
    step = {"x": 32, "y": 8, "z": 2, "core": 1}[axis] * bit
    return permute_devices(x, lambda i: i ^ step)


def turn_y(x, by):
    return permute_devices(x, lambda i: i - i % 32 + (i % 32 + 8 * by) % 32)


def sum_over_devices(x):
    shape = x.shape
    part = x.reshape(512, 256)
    col = lax.axis_index("col")
    core, me = col % 2, col // 8
    give = jnp.where(core == 1, part[:256], part[256:])
    other = swap(give, "core", 1)
    part = jnp.where(core == 1, part[256:], part[:256]) + other
    total = lax.dynamic_slice_in_dim(part, me * 64, 64)
    for by in (1, 2, 3):
        block = lax.dynamic_slice_in_dim(part, (me + by) % 4 * 64, 64)
        other = turn_y(block, by)
        total = total + other
    part = total
    for axis in ("x", "z"):
        for bit in (1, 2):
            other = swap(part, axis, bit)
            part = lax.optimization_barrier(part + other)
    joined = lax.dynamic_update_slice_in_dim(jnp.zeros((256, 256), F32), part, me * 64, 0)
    for by in (1, 2, 3):
        other = turn_y(part, by)
        joined = lax.dynamic_update_slice_in_dim(joined, other, (me - by) % 4 * 64, 0)
    other = swap(joined, "core", 1)
    both = jnp.concatenate([joined, other]), jnp.concatenate([other, joined])
    return jnp.where(core == 1, both[1], both[0]).reshape(shape)


def work(tiles, probe_wave, propagator_phase, positions, slot_count, intensity):
    layers = tiles.shape[0]
    slots = positions.shape[0]
    last = layers - 1
    strip = tiles[0, :, :WIN]
    lowers = [shift(strip, "row", -1)]
    rest, strip = lax.optimization_barrier((tiles, strip))
    first = rest[0]
    rights = [shift(first, "col", -1)]
    rest, first = lax.optimization_barrier((rest, first))
    for layer in range(1, layers):
        lowers.append(shift(rest[layer, :, :WIN], "row", -1))
        rights.append(shift(rest[layer], "col", -1))
    tab = dft_tables()
    phase = parity_order(propagator_phase).reshape(2, 1, HALF, WIN)
    kern = jnp.concatenate([jnp.cos(phase), jnp.sin(phase)], axis=1)
    measured = parity_order(intensity).reshape(slots, 2, HALF, WIN)
    sides = []
    for layer in range(layers):
        sides.append((rights[layer], shift(lowers[layer], "col", -1)))
    waves = [probe_wave[None]]
    slabs = []
    for layer in range(last):
        slab, wave = run_forward(
            layer, slots, positions, tiles, lowers[layer], sides[layer], waves[layer], tab, kern
        )
        slabs.append(slab)
        waves.append(wave)
    grads = [None] * layers
    *grads[last], g_wave = run_turn(
        last, slots, positions, slot_count, tiles, lowers[last], sides[last], waves[last],
        tab, measured
    )
    for layer in reversed(range(last)):
        *grads[layer], g_wave = run_backward(
            slots, positions, slabs[layer], waves[layer], g_wave, tab, kern, layer == 0
        )
    outs = [None] * layers
    for layer in reversed(range(layers)):
        own, lower, *side = grads[layer]
        if layer:
            back = shift(side[0], "col", 1)
            right, corner = back[:, :512], back[:, 512:]
        else:
            corner = shift(side[1], "col", 1)
            right = shift(side[0], "col", 1)
        below = shift(lower + corner, "row", 1)
        outs[layer] = (own + right).at[:, :WIN].add(below)
    probe = sum_over_devices(g_wave[0])
    return (jnp.stack(outs), probe)


def solution(mesh):
    placed = (
        P(None, None, "row", "col"),
        P(),
        P(),
        P(("row", "col"), None),
        P(("row", "col")),
        P(("row", "col"), None, None),
    )
    return jax.shard_map(
        work,
        mesh=mesh,
        in_specs=placed,
        out_specs=(P(None, None, "row", "col"), P()),
        check_vma=False,
    )
```

```python
import functools
import math

import jax
import jax.numpy as jnp
import numpy as np
from jax import lax
from jax.experimental import pallas as pl
from jax.experimental.pallas import tpu as pltpu
from jax.sharding import PartitionSpec as P


WIN = 256
HALF = 128
F32 = jnp.float32
BF16 = jnp.bfloat16


def shift(x, axis, by):
    devices = lax.axis_size(axis)
    pairs = [(i, i + by) for i in range(devices) if 0 <= i + by < devices]
    return lax.ppermute(x, axis, pairs)


def dft_tables():
    n = np.arange(HALF)
    even = 2.0 * math.pi * ((2 * np.outer(n, n)) % WIN) / WIN
    odd = 2.0 * math.pi * ((np.outer(n, 2 * n + 1)) % WIN) / WIN
    tables = []
    for angle in (even, odd):
        cos, sin = np.cos(angle) / 16.0, np.sin(angle) / 16.0
        tables.append(np.block([[cos, -sin], [sin, cos]]))
    whole = np.stack(tables).astype(np.float32)
    high = whole.astype(jnp.bfloat16)
    low = (whole - high.astype(np.float32)).astype(jnp.bfloat16)
    held = lax.optimization_barrier(jnp.asarray(np.stack([high, low], axis=1)))
    return jnp.stack([held, held.transpose(0, 1, 3, 2)], axis=1).reshape(4, 2, WIN, WIN)


def split(x):
    high = x.astype(BF16)
    low = (x - high.astype(F32)).astype(BF16)
    return high, low


def right_mul(x, tab, index):
    high, low = split(x)
    t_high, t_low = tab[index, 0], tab[index, 1]
    return jnp.dot(
        jnp.concatenate([high, low, high], axis=1),
        jnp.concatenate([t_high, t_high, t_low], axis=0),
        preferred_element_type=F32,
    )


def left_mul(x, tab, index):
    high, low = split(x)
    t_high, t_low = tab[index, 0], tab[index, 1]
    return jnp.dot(
        jnp.concatenate([t_high, t_high, t_low], axis=1),
        jnp.concatenate([high, low, high], axis=0),
        preferred_element_type=F32,
    )


EVEN, EVEN_T, ODD, ODD_T = range(4)


def forward2d(re, im, tab):
    re0, re1, im0, im1 = re[:, :HALF], re[:, HALF:], im[:, :HALF], im[:, HALF:]
    even = right_mul(jnp.concatenate([re0 + re1, im0 + im1], axis=1), tab, EVEN)
    odd = right_mul(jnp.concatenate([re0 - re1, im0 - im1], axis=1), tab, ODD)
    re = jnp.concatenate([even[:, :HALF], odd[:, :HALF]], axis=1)
    im = jnp.concatenate([even[:, HALF:], odd[:, HALF:]], axis=1)
    re0, re1, im0, im1 = re[:HALF], re[HALF:], im[:HALF], im[HALF:]
    even = left_mul(jnp.concatenate([re0 + re1, im0 + im1], axis=0), tab, EVEN_T)
    odd = left_mul(jnp.concatenate([re0 - re1, im0 - im1], axis=0), tab, ODD_T)
    return even, odd


def inverse2d(even, odd, tab):
    a = left_mul(even, tab, EVEN)
    b = left_mul(odd, tab, ODD)
    plus, minus = a + b, a - b
    re = jnp.concatenate([plus[:HALF], minus[:HALF]], axis=0)
    im = jnp.concatenate([plus[HALF:], minus[HALF:]], axis=0)
    a = right_mul(jnp.concatenate([re[:, :HALF], im[:, :HALF]], axis=1), tab, EVEN_T)
    b = right_mul(jnp.concatenate([re[:, HALF:], im[:, HALF:]], axis=1), tab, ODD_T)
    plus, minus = a + b, a - b
    re = jnp.concatenate([plus[:, :HALF], minus[:, :HALF]], axis=1)
    im = jnp.concatenate([plus[:, HALF:], minus[:, HALF:]], axis=1)
    return re, im


def propagate(re, im, tab, kern, sign):
    halves = forward2d(re, im, tab)
    moved = []
    for parity in range(2):
        f_re, f_im = halves[parity][:HALF], halves[parity][HALF:]
        k_re, k_im = kern[parity, 0], kern[parity, 1] * sign
        moved.append(
            jnp.concatenate([k_re * f_re - k_im * f_im, k_re * f_im + k_im * f_re], axis=0)
        )
    return inverse2d(moved[0], moved[1], tab)


def far_adjoint(re, im, tab, measured, used):
    halves = forward2d(re, im, tab)
    moved = []
    for parity in range(2):
        f_re, f_im = halves[parity][:HALF], halves[parity][HALF:]
        weight = (f_re * f_re + f_im * f_im - measured[0, parity]) * used
        moved.append(jnp.concatenate([weight * f_re, weight * f_im], axis=0))
    return inverse2d(moved[0], moved[1], tab)


def cut(ext, part, row, col):
    base = col // HALF
    lane = col % HALF
    keep = lax.broadcasted_iota(jnp.int32, (WIN, HALF), 1) < HALF - lane
    back = (HALF - lane) % HALF
    turned = [pltpu.roll(ext[part, base + j, pl.ds(row, WIN), :], back, 1) for j in range(3)]
    return jnp.concatenate(
        [jnp.where(keep, turned[0], turned[1]), jnp.where(keep, turned[1], turned[2])], axis=1
    )


def add_back(ext, part, row, col, value):
    base = col // HALF
    lane = col % HALF
    keep = lax.broadcasted_iota(jnp.int32, (WIN, HALF), 1) >= lane
    zero = jnp.zeros((WIN, HALF), F32)
    turned = [pltpu.roll(value[:, j * HALF : (j + 1) * HALF], lane, 1) for j in range(2)]
    wide = [
        jnp.where(keep, turned[0], zero),
        jnp.where(keep, turned[1], turned[0]),
        jnp.where(keep, zero, turned[1]),
    ]
    for j in range(3):
        place = (part, base + j, pl.ds(row, WIN), slice(None))
        ext[place] = ext[place] + wide[j]


def gather_ext(own, lower, sides, ext):
    for j in range(2):
        lanes = slice(j * HALF, (j + 1) * HALF)
        ext[:, j, :512] = own[0, :, :, lanes]
        ext[:, j, 512:] = lower[:, :, lanes]
        top = 0
        for side in sides:
            rows = side.shape[1]
            ext[:, 2 + j, top : top + rows] = side[:, :, lanes]
            top += rows


def spread_ext(ext, own, lower, sides):
    for j in range(2):
        lanes = slice(j * HALF, (j + 1) * HALF)
        own[:, :, lanes] = ext[:, j, :512]
        lower[:, :, lanes] = ext[:, j, 512:]
        top = 0
        for side in sides:
            rows = side.shape[1]
            side[:, :, lanes] = ext[:, 2 + j, top : top + rows]
            top += rows


def forward_kernel(side_count, pos, own, lower, *refs):
    sides, (wave, tab, kern, slab_out, wave_out, ext) = refs[:side_count], refs[side_count:]
    slot = pl.program_id(0)

    @pl.when(slot == 0)
    def _():
        gather_ext(own, lower, sides, ext)

    row, col = pos[slot, 0], pos[slot, 1]
    s_re, s_im = cut(ext, 0, row, col), cut(ext, 1, row, col)
    slab_out[0, 0], slab_out[0, 1] = s_re, s_im
    w_re, w_im = wave[0, 0], wave[0, 1]
    wave_out[0, 0], wave_out[0, 1] = propagate(
        w_re * s_re - w_im * s_im, w_re * s_im + w_im * s_re, tab, kern, 1.0
    )


def turn_kernel(side_count, pos, count, own, lower, *refs):
    sides, (wave, tab, measured, g_own, g_lower, g_side, g_wave, ext, g_ext) = (
        refs[:side_count], refs[side_count:]
    )
    slot = pl.program_id(0)

    @pl.when(slot == 0)
    def _():
        gather_ext(own, lower, sides, ext)
        g_ext[...] = jnp.zeros(g_ext.shape, F32)

    row, col = pos[slot, 0], pos[slot, 1]
    used = jnp.where(slot < count[0], 1.0, 0.0).astype(F32)
    s_re, s_im = cut(ext, 0, row, col), cut(ext, 1, row, col)
    w_re, w_im = wave[0, 0], wave[0, 1]
    e_re, e_im = far_adjoint(
        w_re * s_re - w_im * s_im, w_re * s_im + w_im * s_re, tab, measured, used
    )
    add_back(g_ext, 0, row, col, w_re * e_re + w_im * e_im)
    add_back(g_ext, 1, row, col, w_re * e_im - w_im * e_re)
    g_wave[0, 0] = s_re * e_re + s_im * e_im
    g_wave[0, 1] = s_re * e_im - s_im * e_re

    @pl.when(slot == pl.num_programs(0) - 1)
    def _():
        spread_ext(g_ext, g_own, g_lower, [g_side])


def backward_kernel(first, pos, slab, wave, g_next, tab, kern, g_own, g_lower, *refs):
    sides, (g_wave, g_ext) = refs[:-2], refs[-2:]
    slot = pl.program_id(0)

    @pl.when(slot == 0)
    def _():
        g_ext[...] = jnp.zeros(g_ext.shape, F32)
        if first:
            g_wave[...] = jnp.zeros(g_wave.shape, F32)

    row, col = pos[slot, 0], pos[slot, 1]
    s_re, s_im = slab[0, 0], slab[0, 1]
    w_re, w_im = wave[0, 0], wave[0, 1]
    e_re, e_im = propagate(g_next[0, 0], g_next[0, 1], tab, kern, -1.0)
    add_back(g_ext, 0, row, col, w_re * e_re + w_im * e_im)
    add_back(g_ext, 1, row, col, w_re * e_im - w_im * e_re)
    p_re = s_re * e_re + s_im * e_im
    p_im = s_re * e_im - s_im * e_re
    if first:
        g_wave[0, 0] += p_re
        g_wave[0, 1] += p_im
    else:
        g_wave[0, 0], g_wave[0, 1] = p_re, p_im

    @pl.when(slot == pl.num_programs(0) - 1)
    def _():
        spread_ext(g_ext, g_own, g_lower, sides)


def whole(*shape):
    return pl.BlockSpec(shape, lambda slot, *_: (0,) * len(shape))


def by_slot(*shape):
    return pl.BlockSpec((1,) + shape, lambda slot, *_: (slot,) + (0,) * len(shape))


TILE = (2, 512, 256)
STRIP = (2, 256, 256)
SIDE = (2, 768, 256)
PARAMS = pltpu.CompilerParams(dimension_semantics=("arbitrary",), vmem_limit_bytes=26 << 20)
COST = pl.CostEstimate(flops=10 * 1000 * 1000 * 1000, bytes_accessed=12 << 20, transcendentals=0)
EXT = pltpu.VMEM((2, 4, 768, HALF), F32)
TABLES = (4, 2, 256, 256)


def arr(*shape):
    return jax.ShapeDtypeStruct(shape, F32)


def tile_of(layer):
    return pl.BlockSpec((1,) + TILE, lambda slot, *_: (layer, 0, 0, 0))


def run_forward(layer, slots, pos, tiles, lower, sides, wave, tab, kern):
    shared = wave.shape[0] == 1
    return pl.pallas_call(
        functools.partial(forward_kernel, len(sides)),
        grid_spec=pltpu.PrefetchScalarGridSpec(
            num_scalar_prefetch=1,
            grid=(slots,),
            in_specs=[tile_of(layer), whole(*STRIP), *[whole(*side.shape) for side in sides],
                      whole(1, *STRIP) if shared else by_slot(*STRIP),
                      whole(*TABLES), whole(2, 2, HALF, WIN)],
            out_specs=[by_slot(*STRIP), by_slot(*STRIP)],
            scratch_shapes=[EXT],
        ),
        out_shape=[arr(slots, *STRIP), arr(slots, *STRIP)],
        compiler_params=PARAMS,
        cost_estimate=COST,
        name="forward",
    )(pos, tiles, lower, *sides, wave, tab, kern)


def run_turn(layer, slots, pos, count, tiles, lower, sides, wave, tab, measured):
    return pl.pallas_call(
        functools.partial(turn_kernel, len(sides)),
        grid_spec=pltpu.PrefetchScalarGridSpec(
            num_scalar_prefetch=2,
            grid=(slots,),
            in_specs=[tile_of(layer), whole(*STRIP), *[whole(*side.shape) for side in sides],
                      by_slot(*STRIP), whole(*TABLES), by_slot(2, HALF, WIN)],
            out_specs=[whole(*TILE), whole(*STRIP), whole(*SIDE), by_slot(*STRIP)],
            scratch_shapes=[EXT, EXT],
        ),
        out_shape=[arr(*TILE), arr(*STRIP), arr(*SIDE), arr(slots, *STRIP)],
        compiler_params=PARAMS,
        cost_estimate=COST,
        name="turn",
    )(pos, count, tiles, lower, *sides, wave, tab, measured)


def run_backward(slots, pos, slab, wave, g_next, tab, kern, first):
    shared = wave.shape[0] == 1
    sides = [TILE, STRIP] if first else [SIDE]
    return pl.pallas_call(
        functools.partial(backward_kernel, first),
        grid_spec=pltpu.PrefetchScalarGridSpec(
            num_scalar_prefetch=1,
            grid=(slots,),
            in_specs=[by_slot(*STRIP), whole(1, *STRIP) if shared else by_slot(*STRIP),
                      by_slot(*STRIP), whole(*TABLES), whole(2, 2, HALF, WIN)],
            out_specs=[whole(*TILE), whole(*STRIP), *[whole(*side) for side in sides],
                       whole(1, *STRIP) if first else by_slot(*STRIP)],
            scratch_shapes=[EXT],
        ),
        out_shape=[arr(*TILE), arr(*STRIP), *[arr(*side) for side in sides],
                   arr(1 if first else slots, *STRIP)],
        compiler_params=PARAMS,
        cost_estimate=COST,
        name="backward",
    )(pos, slab, wave, g_next, tab, kern)


def parity_order(x):
    place = lax.broadcasted_iota(jnp.int32, (WIN, WIN), 0)
    source = lax.broadcasted_iota(jnp.int32, (WIN, WIN), 1)
    pick = (source == place % HALF * 2 + place // HALF).astype(F32)
    high = lax.Precision.HIGHEST
    x = jnp.einsum("...rc,dc->...rd", x, pick, precision=high)
    return jnp.einsum("er,...rd->...ed", pick, x, precision=high)


def permute_devices(x, there):
    count = lax.axis_size("row") * 32
    return lax.ppermute(x, ("row", "col"), [(i, there(i)) for i in range(count)])


def swap(x, axis, bit):
    step = {"x": 32, "y": 8, "z": 2, "core": 1}[axis] * bit
    return permute_devices(x, lambda i: i ^ step)


def turn_y(x, by):
    return permute_devices(x, lambda i: i - i % 32 + (i % 32 + 8 * by) % 32)


def sum_over_devices(x):
    shape = x.shape
    part = x.reshape(512, 256)
    col = lax.axis_index("col")
    core, me = col % 2, col // 8
    give = jnp.where(core == 1, part[:256], part[256:])
    other = swap(give, "core", 1)
    part = jnp.where(core == 1, part[256:], part[:256]) + other
    total = lax.dynamic_slice_in_dim(part, me * 64, 64)
    for by in (1, 2, 3):
        block = lax.dynamic_slice_in_dim(part, (me + by) % 4 * 64, 64)
        other = turn_y(block, by)
        total = total + other
    part = total
    for axis in ("x", "z"):
        for bit in (1, 2):
            other = swap(part, axis, bit)
            part = lax.optimization_barrier(part + other)
    joined = lax.dynamic_update_slice_in_dim(jnp.zeros((256, 256), F32), part, me * 64, 0)
    for by in (1, 2, 3):
        other = turn_y(part, by)
        joined = lax.dynamic_update_slice_in_dim(joined, other, (me - by) % 4 * 64, 0)
    other = swap(joined, "core", 1)
    both = jnp.concatenate([joined, other]), jnp.concatenate([other, joined])
    return jnp.where(core == 1, both[1], both[0]).reshape(shape)


def corner_by_row(right, lower):
    rows, cols = lax.axis_size("row"), lax.axis_size("col")
    up = [((r + 1) * cols + c, r * cols + c) for r in range(rows - 1) for c in range(1, cols, 2)]
    near = [(r * cols + c + 1, r * cols + c) for r in range(rows) for c in range(0, cols, 2)]
    from_below = lax.ppermute(right[:, :WIN], ("row", "col"), up)
    from_core = lax.ppermute(lower, ("row", "col"), near)
    return jnp.where(lax.axis_index("col") % 2 == 1, from_below, from_core)


def work(tiles, probe_wave, propagator_phase, positions, slot_count, intensity):
    layers = tiles.shape[0]
    slots = positions.shape[0]
    last = layers - 1
    first = tiles[0]
    rights = [shift(first, "col", -1)]
    rest, first = lax.optimization_barrier((tiles, first))
    strip = rest[0, :, :WIN]
    lowers = [shift(strip, "row", -1)]
    rest, strip = lax.optimization_barrier((rest, strip))
    for layer in range(1, layers):
        rights.append(shift(rest[layer], "col", -1))
        lowers.append(shift(rest[layer, :, :WIN], "row", -1))
    tab = dft_tables()
    phase = parity_order(propagator_phase).reshape(2, 1, HALF, WIN)
    kern = jnp.concatenate([jnp.cos(phase), jnp.sin(phase)], axis=1)
    measured = parity_order(intensity).reshape(slots, 2, HALF, WIN)
    sides = []
    for layer in range(layers):
        if layer == 1:
            corner = corner_by_row(rights[layer], lowers[layer])
        else:
            corner = shift(lowers[layer], "col", -1)
        sides.append((rights[layer], corner))
    waves = [probe_wave[None]]
    slabs = []
    for layer in range(last):
        slab, wave = run_forward(
            layer, slots, positions, tiles, lowers[layer], sides[layer], waves[layer], tab, kern
        )
        slabs.append(slab)
        waves.append(wave)
    grads = [None] * layers
    *grads[last], g_wave = run_turn(
        last, slots, positions, slot_count, tiles, lowers[last], sides[last], waves[last],
        tab, measured
    )
    for layer in reversed(range(last)):
        *grads[layer], g_wave = run_backward(
            slots, positions, slabs[layer], waves[layer], g_wave, tab, kern, layer == 0
        )
    outs = [None] * layers
    for layer in reversed(range(layers)):
        own, lower, *side = grads[layer]
        if layer:
            back = shift(side[0], "col", 1)
            right, corner = back[:, :512], back[:, 512:]
        else:
            corner = shift(side[1], "col", 1)
            right = shift(side[0], "col", 1)
        below = shift(lower + corner, "row", 1)
        outs[layer] = (own + right).at[:, :WIN].add(below)
    probe = sum_over_devices(g_wave[0])
    return (jnp.stack(outs), probe)


def solution(mesh):
    placed = (
        P(None, None, "row", "col"),
        P(),
        P(),
        P(("row", "col"), None),
        P(("row", "col")),
        P(("row", "col"), None, None),
    )
    return jax.shard_map(
        work,
        mesh=mesh,
        in_specs=placed,
        out_specs=(P(None, None, "row", "col"), P()),
        check_vma=False,
    )
```
